32 devices in a mesh: groups: 2 (over y), blocks: 8 (over z, x), inst: 2 (over core).
Axes of the slice: x: 2, y: 2, z: 4, core: 2. Of those that a mesh axis runs over, the one named last changes fastest.
Arguments:
- adjoint_start: float32 [32, 6, 16, 8, 128], P(('groups', 'inst'), None, 'blocks'), parts along dimension 0, may hold values from -6 to 6
- objective_grad: float32 [32, 6, 16, 8, 128], P(('groups', 'inst'), None, 'blocks'), parts along dimension 0, may hold values from -6 to 6
- diag_inverse: float32 [32, 6, 6, 16, 8, 128], P(('groups', 'inst'), None, None, 'blocks'), parts along dimension 0, may hold values from -0.1 to 0.5, as said below
- face_coupling: float32 [32, 6, 16, 8, 128], P(('groups', 'inst'), None, 'blocks'), parts along dimension 0, may hold values from 0.05 to 0.5
- surface_index: int32 [4096], P(('groups', 'blocks')), parts along dimension 0, may hold values from 0 to 2047
- wall_point_partials: float32 [32, 3, 6, 2048], P(('groups', 'inst'), None, None, 'blocks'), parts along dimension 0, may hold values from -0.625 to 0.625
Outputs:
- adjoint: float32 [32, 6, 16, 8, 128], P(('groups', 'inst'), None, 'blocks'), parts along dimension 0
- sensitivity: float32 [3, 4096], P(None, ('groups', 'blocks')), parts along dimension 1
The draws below stay inside these ranges and needn't reach their ends.
There are 2 independent parts, one for each index of `groups`. The reference program is written for one: setup_inputs(seed, part) draws one part's arguments, and reference() takes and returns one part's arrays. A program takes and returns all parts, laid end to end along the dimension named above; each array names one. Nothing has to cross between parts.
Inputs may be any that keep to these rules, and one draw needn't show every extreme that they name: `surface_index`: each entry is a cell of its own block. `diag_inverse`: each 6 x 6 block has diagonal entries between 0.25 and 0.5.
All inputs are finite; a program needn't handle non-finite values.
Results may differ from the reference program's by a relative error of at most 0.0001.
Values sent between devices are 32-bit elements; how exact they have to be, the bound alone decides.
No kernel may reach another device: no remote copies, remote signals or barrier semaphores. Data moves between devices by JAX's collectives and lax.ppermute only.
A program may use at most 64 MiB of HBM per device.

```python
import math
import jax
import jax.numpy as jnp
from jax import lax

NINST = 16
VARS = 6
CI = 2
CR = 8
CA = 128
SURF = 256
SWEEPS = 4
NCIRC = 16
SURFACE = 2048


def draw_diag_inverse(key, part):
    shape = (NINST, VARS, VARS, NCIRC, CR, CA)
    diag_key = jax.random.fold_in(key, 11)
    off_key = jax.random.fold_in(key, 12)
    low = jnp.log(jnp.float32(0.25))
    high = jnp.log(jnp.float32(0.5))
    diagonal = jnp.exp(jax.random.uniform(diag_key, shape, jnp.float32, low, high))
    offdiag = jnp.clip(0.05 * jax.random.normal(off_key, shape, jnp.float32), -0.1, 0.1)
    identity = jnp.eye(VARS, dtype=jnp.float32)[None, :, :, None, None, None]
    return identity * diagonal + (1.0 - identity) * offdiag


def place_ends(array, own_key, low, top_value):
    index_at = [jax.random.randint(jax.random.fold_in(own_key, axis), (), 0, length) for axis, length in enumerate(array.shape)]
    longest = array.shape.index(max(array.shape))
    neighbour = index_at[:longest] + [(index_at[longest] + 1) % array.shape[longest]] + index_at[longest + 1:]
    return array.at[tuple(index_at)].set(low).at[tuple(neighbour)].set(top_value)


def levels(rng, dims, pieces, least, largest):
    def one(axis_at, blocks):
        draws = jax.random.uniform(jax.random.fold_in(jax.random.fold_in(rng, 6), axis_at), (blocks,), jnp.float32, least / len(pieces), largest / len(pieces))
        return jnp.repeat(jnp.exp(draws), dims[axis_at] // blocks).reshape((-1,) + (1,) * (len(dims) - axis_at - 1))

    loudness = one(*pieces[0])
    for cut in pieces[1:]:
        loudness = loudness * one(*cut)
    return loudness


def noise(rng, shape, width, bound, split=(), kind=jnp.bfloat16):
    loudness = levels(rng, shape, split, -0.22, 0.18) if split else 1.0
    result = jax.random.normal(rng, shape, jnp.float32) * width * loudness
    return jnp.minimum(jnp.maximum(result, -bound), bound).astype(kind)


def setup_inputs(seed: int = 0, part: int = 0) -> dict:
    key_list = jax.random.split(jax.random.key(seed), 7)
    part_splits = jax.random.split(jax.random.fold_in(key_list[6], part), 7)
    adjoint_start = noise(part_splits[0], (NINST, VARS, NCIRC, CR, CA), 1.0, 6.0, ((0, 2), (2, 8)), jnp.float32)
    objective_grad = noise(part_splits[1], (NINST, VARS, NCIRC, CR, CA), 1.0, 6.0, ((0, 2), (2, 8)), jnp.float32)
    diag_inverse = draw_diag_inverse(jax.random.fold_in(jax.random.fold_in(key_list[6], part), 71), part)
    face_coupling = jnp.clip(jnp.exp(math.log(0.5) - 2.3025851 * jax.random.uniform(part_splits[3], (NINST, 6, NCIRC, CR, CA), jnp.float32) ** levels(part_splits[3], (NINST, 6, NCIRC, CR, CA), ((0, 2), (2, 8)), -0.2, 0.2)), 0.05, 0.5)
    surface_index = place_ends(jax.random.randint(part_splits[4], (SURFACE,), 0, CI * CR * CA), jax.random.fold_in(part_splits[4], 1), 0, (CI * CR * CA) - 1).astype(jnp.int32)
    wall_point_partials = noise(part_splits[5], (NINST, 3, VARS, SURFACE), (VARS * NINST) ** -0.5, 0.625, ((0, 2), (3, 8)), jnp.float32)
    return dict(adjoint_start=adjoint_start, objective_grad=objective_grad, diag_inverse=diag_inverse, face_coupling=face_coupling, surface_index=surface_index, wall_point_partials=wall_point_partials)


spectral_weight = 0.25


def spectral_matrix(number):
    indices = jnp.arange(number, dtype=jnp.int32)
    distance = (indices[:, None] - indices[None, :]) % number
    angle = jnp.pi * distance.astype(jnp.float32) / number
    color_parity = (1 - 2 * (distance % 2)).astype(jnp.float32)
    sine = jnp.where(distance == 0, jnp.float32(1.0), jnp.sin(angle))
    value_entries = jnp.where(distance == 0, jnp.float32(0.0), 0.5 * color_parity * jnp.cos(angle) / sine)
    return value_entries * spectral_weight


def displace(field, mesh_axis_count, amount):
    widths = [(0, 0)] * field.ndim
    length = field.shape[mesh_axis_count]
    if amount > 0:
        widths[mesh_axis_count] = (1, 0)
        padded = jnp.pad(field, widths)
        return lax.slice_in_dim(padded, 0, length, axis=mesh_axis_count)
    widths[mesh_axis_count] = (0, 1)
    padded = jnp.pad(field, widths)
    return lax.slice_in_dim(padded, 1, length + 1, axis=mesh_axis_count)


def neighbours(center, below, above, coupling):
    total = coupling[:, 0:1] * below + coupling[:, 1:2] * above
    total = total + coupling[:, 2:3] * displace(center, 3, 1) + coupling[:, 3:4] * displace(center, 3, -1)
    total = total + coupling[:, 4:5] * displace(center, 4, 1) + coupling[:, 5:6] * displace(center, 4, -1)
    return total


def sweep_update(objective_grad, diag_inverse, coupled_terms, spectral_term):
    resid = objective_grad + coupled_terms - spectral_term
    return jnp.einsum('nuvira,nuira->nvira', diag_inverse, resid, precision=lax.Precision.HIGHEST)


def reference(adjoint_start, objective_grad, diag_inverse, face_coupling, surface_index, wall_point_partials):
    spectral = spectral_matrix(NINST)
    adjoint = adjoint_start
    for repeat in range(SWEEPS):
        below = jnp.roll(adjoint, 1, axis=2)
        above = jnp.roll(adjoint, -1, axis=2)
        coupled_terms = neighbours(adjoint, below, above, face_coupling)
        spectral_term = jnp.einsum('mn,mvira->nvira', spectral, adjoint, precision=lax.Precision.HIGHEST)
        adjoint = sweep_update(objective_grad, diag_inverse, coupled_terms, spectral_term)
    cells = CR * CA
    owners = jnp.arange(SURFACE, dtype=jnp.int32) // SURF
    circ_index = owners * CI + surface_index // cells
    remainder = surface_index % cells
    selected_entries = adjoint[:, :, circ_index, remainder // CA, remainder % CA]
    sensitivity = jnp.einsum('fex,fpex->px', selected_entries, wall_point_partials, precision=lax.Precision.HIGHEST)
    return adjoint, sensitivity
```

```python
import math

import jax
import jax.numpy as jnp
from jax import lax
from jax.experimental import pallas as pl
from jax.experimental.pallas import tpu as pltpu
from jax.sharding import PartitionSpec as P

SWEEPS = 4
SPECTRAL_WEIGHT = 0.25


def spectral_values(number):
    values = [0.0]
    for k in range(1, number):
        angle = math.pi * k / number
        values.append(SPECTRAL_WEIGHT * 0.5 * (-1) ** k * math.cos(angle) / math.sin(angle))
    return values


def update_layer(layer, own, partner, inner, halo, grad, diag, coupling, new, masked, resid):
    inst, variables, radial, axial = own.shape
    values = spectral_values(2 * inst)
    rows = lax.broadcasted_iota(jnp.int32, (radial, axial), 0)
    lanes = lax.broadcasted_iota(jnp.int32, (radial, axial), 1)
    edges = (rows > 0, rows < radial - 1, lanes > 0, lanes < axial - 1)
    for n in range(inst):
        for d, inside in enumerate(edges):
            masked[n, d] = jnp.where(inside, coupling[n, 2 + d, layer], 0.0)
    for u in range(variables):
        cycle = [own[m, u] for m in range(inst)] + [partner[m, u] for m in range(inst)]
        for n in range(inst):
            center = cycle[n]
            total = grad[n, u, layer]
            total = total + coupling[n, layer, layer] * halo[n, u]
            total = total + coupling[n, 1 - layer, layer] * inner[n, u]
            total = total + masked[n, 0] * pltpu.roll(center, 1, 0)
            total = total + masked[n, 1] * pltpu.roll(center, radial - 1, 0)
            total = total + masked[n, 2] * pltpu.roll(center, 1, 1)
            total = total + masked[n, 3] * pltpu.roll(center, axial - 1, 1)
            term = values[inst] * cycle[n + inst]
            for k in range(1, inst):
                term = term + values[k] * (cycle[(n + k) % (2 * inst)] - cycle[(n - k) % (2 * inst)])
            resid[n, u] = total - term
    for n in range(inst):
        terms = [resid[n, u] for u in range(variables)]
        for v in range(variables):
            total = diag[n, 0, v, layer] * terms[0]
            for u in range(1, variables):
                total = total + diag[n, u, v, layer] * terms[u]
            new[n, v] = total


def layer_sensitivity(layer, values, index, partials):
    inst, variables, radial, axial = values.shape
    surface = index.shape[1]
    place = index[...]
    lane = place % axial
    row = (place // axial) % radial
    select = lax.broadcasted_iota(jnp.int32, (axial, surface), 0) == jnp.broadcast_to(lane, (axial, surface))
    select = select.astype(jnp.float32).astype(jnp.bfloat16)
    here = (lax.broadcasted_iota(jnp.int32, (radial, surface), 0) == jnp.broadcast_to(row, (radial, surface))) & (
        jnp.broadcast_to(place // (axial * radial), (radial, surface)) == layer
    )
    flat = values[...].reshape(inst * variables * radial, axial)
    high = flat.astype(jnp.bfloat16)
    rest = flat - high.astype(jnp.float32)
    middle = rest.astype(jnp.bfloat16)
    low = (rest - middle.astype(jnp.float32)).astype(jnp.bfloat16)
    picked = jnp.dot(
        jnp.concatenate([high, middle, low], axis=1),
        jnp.concatenate([select, select, select], axis=0),
        preferred_element_type=jnp.float32,
    )
    sums = [jnp.zeros((radial, surface), jnp.float32) for _ in range(partials.shape[0])]
    for n in range(inst):
        for v in range(variables):
            start = (n * variables + v) * radial
            part = picked[start : start + radial]
            for k in range(len(sums)):
                sums[k] = sums[k] + part * jnp.broadcast_to(partials[k, v, n : n + 1, :], (radial, surface))
    return [jnp.sum(jnp.where(here, s, 0.0), axis=0, keepdims=True) for s in sums]


def sweep_kernel(layer_ref, own, partner, inner, halo, grad, diag, coupling, new, masked, resid):
    update_layer(layer_ref[0], own, partner, inner, halo, grad, diag, coupling, new, masked, resid)


def first_kernel(
    layer_ref, own, partner, inner, halo, grad, diag, coupling, index, partials, new, sens, masked, resid
):
    layer = layer_ref[0]
    update_layer(layer, own, partner, inner, halo, grad, diag, coupling, new, masked, resid)
    for k, row in enumerate(layer_sensitivity(layer, new, index, partials)):
        sens[k : k + 1, :] = row


def last_kernel(
    layer_ref,
    own,
    partner,
    inner,
    halo,
    grad,
    diag,
    coupling,
    index,
    partials,
    done,
    done_sens,
    adjoint,
    sens,
    new,
    masked,
    resid,
):
    layer = layer_ref[0]
    update_layer(layer, own, partner, inner, halo, grad, diag, coupling, new, masked, resid)
    for n in range(own.shape[0]):
        for v in range(own.shape[1]):
            adjoint[n, v, layer] = new[n, v]
            adjoint[n, v, 1 - layer] = done[n, v]
    for k, row in enumerate(layer_sensitivity(layer, new, index, partials)):
        sens[k : k + 1, :] = done_sens[k : k + 1, :] + row


def call(kernel, out_shapes, operands, scratch=()):
    inst, variables, radial, axial = operands[1].shape
    vmem = pl.BlockSpec(memory_space=pltpu.VMEM)
    return pl.pallas_call(
        kernel,
        out_shape=[jax.ShapeDtypeStruct(s, jnp.float32) for s in out_shapes],
        in_specs=[pl.BlockSpec(memory_space=pltpu.SMEM)] + [vmem] * (len(operands) - 1),
        out_specs=[vmem] * len(out_shapes),
        scratch_shapes=list(scratch)
        + [
            pltpu.VMEM((inst, 4, radial, axial), jnp.float32),
            pltpu.VMEM((inst, variables, radial, axial), jnp.float32),
        ],
        compiler_params=pltpu.CompilerParams(vmem_limit_bytes=24 * 1024 * 1024),
    )(*operands)


def body(
    adjoint_start, objective_grad, diag_inverse, face_coupling, surface_index, wall_point_partials
):
    count = lax.axis_size("blocks")
    assert count % 2 == 0 and lax.axis_size("inst") == 2 and adjoint_start.shape[2] == 2
    even_pairs = [(i, i ^ 1) for i in range(count)]
    odd_pairs = [(i, (((i + 1) ^ 1) - 1) % count) for i in range(count)]
    even_layer = 1 - lax.axis_index("blocks") % 2
    odd_layer = 1 - even_layer
    even_ref = even_layer.astype(jnp.int32).reshape(1)
    odd_ref = odd_layer.astype(jnp.int32).reshape(1)
    index = surface_index.reshape(1, -1)
    partials = jnp.transpose(wall_point_partials, (1, 2, 0, 3))

    def swap(layer, pairs):
        return lax.ppermute(layer, "blocks", pairs)

    def cores(layer):
        return lax.ppermute(layer, "inst", [(0, 1), (1, 0)])

    even = lax.dynamic_index_in_dim(adjoint_start, even_layer, 2, keepdims=False)
    odd = lax.dynamic_index_in_dim(adjoint_start, odd_layer, 2, keepdims=False)
    shape = even.shape
    fixed = (objective_grad, diag_inverse, face_coupling)
    for sweep in range(SWEEPS):
        even_halo = swap(even, even_pairs)
        odd_halo = swap(odd, odd_pairs)
        even_partner = cores(even)
        odd_partner = cores(odd)
        even_args = (even_ref, even, even_partner, odd, even_halo, *fixed)
        odd_args = (odd_ref, odd, odd_partner, even, odd_halo, *fixed)
        if sweep < SWEEPS - 1:
            (even,) = call(sweep_kernel, [shape], even_args)
            (odd,) = call(sweep_kernel, [shape], odd_args)
    sens_shape = (partials.shape[0], surface_index.shape[0])
    even, sens = call(first_kernel, [shape, sens_shape], (*even_args, index, partials))
    adjoint, sens = call(
        last_kernel,
        [adjoint_start.shape, sens_shape],
        (*odd_args, index, partials, even, sens),
        [pltpu.VMEM(shape, jnp.float32)],
    )
    return adjoint, sens + cores(sens)


def solution(mesh):
    return jax.shard_map(
        body,
        mesh=mesh,
        in_specs=(
            P(("groups", "inst"), None, "blocks", None, None),
            P(("groups", "inst"), None, "blocks", None, None),
            P(("groups", "inst"), None, None, "blocks", None, None),
            P(("groups", "inst"), None, "blocks", None, None),
            P(("groups", "blocks")),
            P(("groups", "inst"), None, None, "blocks"),
        ),
        out_specs=(
            P(("groups", "inst"), None, "blocks", None, None),
            P(None, ("groups", "blocks")),
        ),
        check_vma=False,
    )
```

```python
import math

import jax
import jax.numpy as jnp
from jax import lax
from jax.experimental import pallas as pl
from jax.experimental.pallas import tpu as pltpu
from jax.sharding import PartitionSpec as P

SWEEPS = 4
CHUNKS = (1, 1)
SPECTRAL_WEIGHT = 0.25


def spectral_values(number):
    values = [0.0]
    for k in range(1, number):
        angle = math.pi * k / number
        values.append(SPECTRAL_WEIGHT * 0.5 * (-1) ** k * math.cos(angle) / math.sin(angle))
    return values


def update_chunk(layer, start, own, partner, inner, halo, grad, diag, coupling, new, masked, resid):
    inst, variables, radial, axial = own.shape
    size = new.shape[0]
    skip = start if halo.shape[0] == inst else 0
    values = spectral_values(2 * inst)
    rows = lax.broadcasted_iota(jnp.int32, (radial, axial), 0)
    lanes = lax.broadcasted_iota(jnp.int32, (radial, axial), 1)
    edges = (rows > 0, rows < radial - 1, lanes > 0, lanes < axial - 1)
    for i in range(size):
        for d, inside in enumerate(edges):
            masked[i, d] = jnp.where(inside, coupling[start + i, 2 + d, layer], 0.0)
    for u in range(variables):
        cycle = [own[m, u] for m in range(inst)] + [partner[m, u] for m in range(inst)]
        for i in range(size):
            n = start + i
            center = cycle[n]
            total = grad[n, u, layer]
            total = total + coupling[n, layer, layer] * halo[skip + i, u]
            total = total + coupling[n, 1 - layer, layer] * inner[n, u]
            total = total + masked[i, 0] * pltpu.roll(center, 1, 0)
            total = total + masked[i, 1] * pltpu.roll(center, radial - 1, 0)
            total = total + masked[i, 2] * pltpu.roll(center, 1, 1)
            total = total + masked[i, 3] * pltpu.roll(center, axial - 1, 1)
            term = values[inst] * cycle[(n + inst) % (2 * inst)]
            for k in range(1, inst):
                term = term + values[k] * (cycle[(n + k) % (2 * inst)] - cycle[(n - k) % (2 * inst)])
            resid[i, u] = total - term
    for i in range(size):
        terms = [resid[i, u] for u in range(variables)]
        for v in range(variables):
            total = diag[start + i, 0, v, layer] * terms[0]
            for u in range(1, variables):
                total = total + diag[start + i, u, v, layer] * terms[u]
            new[i, v] = total


def chunk_sensitivity(layer, start, values, index, partials):
    inst, variables, radial, axial = values.shape
    surface = index.shape[1]
    place = index[...]
    lane = place % axial
    row = (place // axial) % radial
    select = lax.broadcasted_iota(jnp.int32, (axial, surface), 0) == jnp.broadcast_to(lane, (axial, surface))
    select = select.astype(jnp.float32).astype(jnp.bfloat16)
    here = (lax.broadcasted_iota(jnp.int32, (radial, surface), 0) == jnp.broadcast_to(row, (radial, surface))) & (
        jnp.broadcast_to(place // (axial * radial), (radial, surface)) == layer
    )
    flat = values[...].reshape(inst * variables * radial, axial)
    high = flat.astype(jnp.bfloat16)
    rest = flat - high.astype(jnp.float32)
    middle = rest.astype(jnp.bfloat16)
    low = (rest - middle.astype(jnp.float32)).astype(jnp.bfloat16)
    picked = jnp.dot(
        jnp.concatenate([high, middle, low], axis=1),
        jnp.concatenate([select, select, select], axis=0),
        preferred_element_type=jnp.float32,
    )
    sums = [jnp.zeros((radial, surface), jnp.float32) for _ in range(partials.shape[0])]
    for n in range(inst):
        for v in range(variables):
            at = (n * variables + v) * radial
            part = picked[at : at + radial]
            for k in range(len(sums)):
                sums[k] = sums[k] + part * jnp.broadcast_to(partials[k, v, start + n : start + n + 1, :], (radial, surface))
    return [jnp.sum(jnp.where(here, s, 0.0), axis=0, keepdims=True) for s in sums]


def own_layer(side):
    odd_block = lax.axis_index("blocks") % 2
    return odd_block if side else 1 - odd_block


def copy_all(pairs, sems):
    copies = [pltpu.make_async_copy(*pair, sems.at[j]) for j, pair in enumerate(pairs)]
    for copy in copies:
        copy.start()
    for copy in copies:
        copy.wait()


def layer_of(source, layer, out, start=0):
    return [(source.at[start + n, :, layer], out.at[n]) for n in range(out.shape[0])]


def first_split(source, out, sems):
    copy_all(layer_of(source, own_layer(0), out), sems)


def load_kernel(grad, diag, coupling, source, after, grad_out, diag_out, coupling_out, whole, *refs):
    *chunks, sems = refs
    layer = own_layer(1)
    pairs = layer_of(source, layer, whole)
    for j, chunk in enumerate(chunks):
        pairs += layer_of(source, layer, chunk, j * chunk.shape[0])
    copy_all(pairs + [(coupling, coupling_out), (grad, grad_out), (diag, diag_out)], sems)


def pack_kernel(even, odd, both):
    both[0] = even[...]
    both[1] = odd[...]


def join_kernel(*refs):
    *chunks, out, sems = refs
    pairs = []
    start = 0
    for chunk in chunks:
        layer = own_layer(0 if start < out.shape[0] else 1)
        first = start % out.shape[0]
        pairs.append((chunk, out.at[pl.ds(first, chunk.shape[0]), :, layer]))
        start += chunk.shape[0]
    copy_all(pairs, sems)


VMEM = pl.BlockSpec(memory_space=pltpu.VMEM)
HBM = pl.BlockSpec(memory_space=pltpu.HBM)
COST = pl.CostEstimate(flops=10**10, transcendentals=0, bytes_accessed=10**8)
PACK_COST = COST
PARAMS = pltpu.CompilerParams(vmem_limit_bytes=24 * 1024 * 1024)


def arrays(*shapes):
    return [jax.ShapeDtypeStruct(s, jnp.float32) for s in shapes]


def sweep_chunk(start, size, side, own, partner, inner, halo, fixed, after, earlier=()):
    def kernel(own, partner, inner, halo, grad, diag, coupling, *refs):
        *refs, masked, resid = refs[len(after) :]
        before, outs = refs[: len(earlier)], refs[len(earlier) :]
        new = outs[0]
        update_chunk(
            own_layer(side), start, own, partner.at[1 - lax.axis_index("inst"), side], inner, halo, grad, diag, coupling, new, masked, resid
        )
        if earlier:
            for j, chunk in enumerate([*before, new]):
                size = chunk.shape[0]
                outs[1][j * size : (j + 1) * size] = chunk[...]

    operands = (own, partner, inner, halo, *fixed, *after, *earlier)
    _, variables, radial, axial = own.shape
    shapes = [(size, variables, radial, axial)] + ([own.shape] if earlier else [])
    return pl.pallas_call(
        kernel,
        out_shape=arrays(*shapes),
        in_specs=[VMEM] * len(operands),
        out_specs=[VMEM] * len(shapes),
        scratch_shapes=[
            pltpu.VMEM((size, 4, radial, axial), jnp.float32),
            pltpu.VMEM((size, variables, radial, axial), jnp.float32),
        ],
        cost_estimate=COST,
        compiler_params=PARAMS,
    )(*operands)


def last_chunk(start, size, side, own, partner, inner, halo, fixed, index, partials, sens):
    def kernel(own, partner, inner, halo, grad, diag, coupling, index, partials, *refs):
        *before, new, out, masked, resid = refs
        layer = own_layer(side)
        update_chunk(layer, start, own, partner.at[1 - lax.axis_index("inst"), side], inner, halo, grad, diag, coupling, new, masked, resid)
        for k, row in enumerate(chunk_sensitivity(layer, start, new, index, partials)):
            out[k : k + 1, :] = before[0][k : k + 1, :] + row if before else row

    operands = (own, partner, inner, halo, *fixed, index, partials, *sens)
    _, variables, radial, axial = own.shape
    return pl.pallas_call(
        kernel,
        out_shape=arrays((size, variables, radial, axial), (partials.shape[0], index.shape[1])),
        in_specs=[VMEM] * len(operands),
        out_specs=[VMEM] * 2,
        scratch_shapes=[
            pltpu.VMEM((size, 4, radial, axial), jnp.float32),
            pltpu.VMEM((size, variables, radial, axial), jnp.float32),
        ],
        cost_estimate=COST,
        compiler_params=PARAMS,
    )(*operands)


def body(
    adjoint_start, objective_grad, diag_inverse, face_coupling, surface_index, wall_point_partials
):
    count = lax.axis_size("blocks")
    assert count % 2 == 0 and lax.axis_size("inst") == 2 and adjoint_start.shape[2] == 2
    inst, variables, _, radial, axial = adjoint_start.shape
    sizes = [inst // c for c in CHUNKS]
    even_pairs = [(i, i ^ 1) for i in range(count)]
    odd_pairs = [(i, (((i + 1) ^ 1) - 1) % count) for i in range(count)]
    index = surface_index.reshape(1, -1)
    partials = jnp.transpose(wall_point_partials, (1, 2, 0, 3))
    layer_shape = (inst, variables, radial, axial)

    def cores(values):
        return lax.ppermute(values, "inst", [(0, 1), (1, 0)])

    def exchange(whole):
        (both,) = pl.pallas_call(
            pack_kernel,
            out_shape=arrays((2,) + layer_shape),
            in_specs=[VMEM] * 2,
            out_specs=[VMEM],
            cost_estimate=PACK_COST,
            compiler_params=PARAMS,
        )(*whole)
        return lax.all_gather(both, "inst", axis=0)

    pairs = (even_pairs, odd_pairs)

    def swap(side, chunks):
        return [lax.ppermute(c, "blocks", pairs[side]) for c in chunks]

    (even,) = pl.pallas_call(
        first_split,
        out_shape=arrays(layer_shape),
        in_specs=[HBM],
        out_specs=[VMEM],
        scratch_shapes=[pltpu.SemaphoreType.DMA((inst,))],
        compiler_params=PARAMS,
    )(pltpu.with_memory_space_constraint(adjoint_start, pltpu.HBM))
    sources = (objective_grad, diag_inverse, face_coupling, adjoint_start)
    chunk_shapes = [(sizes[1],) + layer_shape[1:]] * (CHUNKS[1] if CHUNKS[1] > 1 else 0)
    *fixed, odd = pl.pallas_call(
        load_kernel,
        out_shape=arrays(*(s.shape for s in sources[:3]), layer_shape, *chunk_shapes),
        in_specs=[HBM] * len(sources) + [VMEM],
        out_specs=[VMEM] * (4 + len(chunk_shapes)),
        scratch_shapes=[pltpu.SemaphoreType.DMA((inst * (2 if chunk_shapes else 1) + 3,))],
        cost_estimate=COST,
        compiler_params=PARAMS,
    )(*(pltpu.with_memory_space_constraint(s, pltpu.HBM) for s in sources), even)
    fixed, odd, chunks = fixed[:3], (fixed + [odd])[3], (fixed + [odd])[4:]
    whole = [even, odd]
    halos = [swap(0, [even]) * CHUNKS[0], swap(1, chunks or [odd])]
    partner = exchange(whole)
    for sweep in range(SWEEPS - 1):
        next_halos, next_whole = [None, None], [None, None]
        for side, size in enumerate(sizes):
            done = []
            for j in range(CHUNKS[side]):
                args = (side, whole[side], partner, whole[1 - side], halos[side][j], fixed)
                after = next_whole[:side]
                new, *next_whole[side] = sweep_chunk(j * size, size, *args, after, done if (j + 1) * size == inst else ())
                done.append(new)
            next_halos[side] = swap(side, done)
            (next_whole[side],) = next_whole[side] or done
        halos, whole = next_halos, next_whole
        partner = exchange(whole)
    sens = ()
    done = []
    for side, size in enumerate(sizes):
        for j in range(CHUNKS[side]):
            args = (side, whole[side], partner, whole[1 - side], halos[side][j], fixed)
            new, *sens = last_chunk(j * size, size, *args, index, partials, sens)
            done.append(new)
    (total,) = sens
    (adjoint,) = pl.pallas_call(
        join_kernel,
        out_shape=arrays(adjoint_start.shape),
        in_specs=[VMEM] * len(done),
        out_specs=[HBM],
        scratch_shapes=[pltpu.SemaphoreType.DMA((len(done),))],
        compiler_params=PARAMS,
    )(*done)
    return adjoint, total + cores(total)


def solution(mesh):
    return jax.shard_map(
        body,
        mesh=mesh,
        in_specs=(
            P(("groups", "inst"), None, "blocks", None, None),
            P(("groups", "inst"), None, "blocks", None, None),
            P(("groups", "inst"), None, None, "blocks", None, None),
            P(("groups", "inst"), None, "blocks", None, None),
            P(("groups", "blocks")),
            P(("groups", "inst"), None, None, "blocks"),
        ),
        out_specs=(
            P(("groups", "inst"), None, "blocks", None, None),
            P(None, ("groups", "blocks")),
        ),
        check_vma=False,
    )
```

```python
import math

import jax
import jax.numpy as jnp
from jax import lax
from jax.experimental import pallas as pl
from jax.experimental.pallas import tpu as pltpu
from jax.sharding import PartitionSpec as P

SWEEPS = 4
SPECTRAL_WEIGHT = 0.25


def spectral_values(number):
    values = [0.0]
    for k in range(1, number):
        angle = math.pi * k / number
        values.append(SPECTRAL_WEIGHT * 0.5 * (-1) ** k * math.cos(angle) / math.sin(angle))
    return values


def local_terms(layer, own, partner, inner, grad, coupling, base, masked):
    inst, variables, radial, axial = own.shape
    values = spectral_values(2 * inst)
    rows = lax.broadcasted_iota(jnp.int32, (radial, axial), 0)
    lanes = lax.broadcasted_iota(jnp.int32, (radial, axial), 1)
    edges = (rows > 0, rows < radial - 1, lanes > 0, lanes < axial - 1)
    for n in range(inst):
        for d, inside in enumerate(edges):
            masked[n, d] = jnp.where(inside, coupling[n, 2 + d, layer], 0.0)
    for u in range(variables):
        cycle = [own[m, u] for m in range(inst)] + [partner[m, u] for m in range(inst)]
        for n in range(inst):
            center = cycle[n]
            total = grad[n, u, layer]
            total = total + coupling[n, 1 - layer, layer] * inner[n, u]
            total = total + masked[n, 0] * pltpu.roll(center, 1, 0)
            total = total + masked[n, 1] * pltpu.roll(center, radial - 1, 0)
            total = total + masked[n, 2] * pltpu.roll(center, 1, 1)
            total = total + masked[n, 3] * pltpu.roll(center, axial - 1, 1)
            term = values[inst] * cycle[n + inst]
            for k in range(1, inst):
                term = term + values[k] * (cycle[(n + k) % (2 * inst)] - cycle[(n - k) % (2 * inst)])
            base[n, u] = total - term


def update_layer(layer, base, halo, diag, coupling, new):
    inst, variables = base.shape[:2]
    for n in range(inst):
        weight = coupling[n, layer, layer]
        terms = [base[n, u] + weight * halo[n, u] for u in range(variables)]
        for v in range(variables):
            total = diag[n, 0, v, layer] * terms[0]
            for u in range(1, variables):
                total = total + diag[n, u, v, layer] * terms[u]
            new[n, v] = total


def layer_sensitivity(layer, values, index, partials):
    inst, variables, radial, axial = values.shape
    surface = index.shape[1]
    place = index[...]
    lane = place % axial
    row = (place // axial) % radial
    select = lax.broadcasted_iota(jnp.int32, (axial, surface), 0) == jnp.broadcast_to(lane, (axial, surface))
    select = select.astype(jnp.float32).astype(jnp.bfloat16)
    here = (lax.broadcasted_iota(jnp.int32, (radial, surface), 0) == jnp.broadcast_to(row, (radial, surface))) & (
        jnp.broadcast_to(place // (axial * radial), (radial, surface)) == layer
    )
    flat = values[...].reshape(inst * variables * radial, axial)
    high = flat.astype(jnp.bfloat16)
    rest = flat - high.astype(jnp.float32)
    middle = rest.astype(jnp.bfloat16)
    low = (rest - middle.astype(jnp.float32)).astype(jnp.bfloat16)
    picked = jnp.dot(
        jnp.concatenate([high, middle, low], axis=1),
        jnp.concatenate([select, select, select], axis=0),
        preferred_element_type=jnp.float32,
    )
    sums = [jnp.zeros((radial, surface), jnp.float32) for _ in range(partials.shape[0])]
    for n in range(inst):
        for v in range(variables):
            at = (n * variables + v) * radial
            part = picked[at : at + radial]
            for k in range(len(sums)):
                sums[k] = sums[k] + part * jnp.broadcast_to(partials[k, v, n : n + 1, :], (radial, surface))
    return [jnp.sum(jnp.where(here, s, 0.0), axis=0, keepdims=True) for s in sums]


def own_layer(side):
    odd_block = lax.axis_index("blocks") % 2
    return odd_block if side else 1 - odd_block


def copy_all(pairs, sems):
    copies = [pltpu.make_async_copy(*pair, sems.at[j]) for j, pair in enumerate(pairs)]
    for copy in copies:
        copy.start()
    for copy in copies:
        copy.wait()


def layer_of(source, side, out):
    return [(source.at[n, :, own_layer(side)], out.at[n]) for n in range(out.shape[0])]


def first_kernel(source, even, sems):
    copy_all(layer_of(source, 0, even), sems)


def load_kernel(grad, diag, coupling, source, after, grad_out, diag_out, coupling_out, odd, sems):
    pairs = [(coupling, coupling_out), (grad, grad_out), (diag, diag_out)]
    copy_all(layer_of(source, 1, odd) + pairs, sems)


def pack_kernel(even, odd, both):
    both[0] = even[...]
    both[1] = odd[...]


def join_kernel(even, odd, out, sems):
    copy_all([(layer, out.at[:, :, own_layer(side)]) for side, layer in enumerate((even, odd))], sems)


VMEM = pl.BlockSpec(memory_space=pltpu.VMEM)
HBM = pl.BlockSpec(memory_space=pltpu.HBM)
COST = pl.CostEstimate(flops=10**10, transcendentals=0, bytes_accessed=10**8)
PARAMS = pltpu.CompilerParams(vmem_limit_bytes=24 * 1024 * 1024)


def call(kernel, shapes, in_specs, operands, scratch=(), out_spec=VMEM):
    return pl.pallas_call(
        kernel,
        out_shape=[jax.ShapeDtypeStruct(s, jnp.float32) for s in shapes],
        in_specs=in_specs,
        out_specs=[out_spec] * len(shapes),
        scratch_shapes=list(scratch),
        cost_estimate=COST,
        compiler_params=PARAMS,
    )(*operands)


def local_kernel(even, odd, both, grad, coupling, base, masked):
    partner = both.at[1 - lax.axis_index("inst"), 0]
    local_terms(own_layer(0), even, partner, odd, grad, coupling, base, masked)


def even_layer(base, halo, fixed, last=None):
    _, diag, coupling = fixed

    def kernel(base, halo, diag, coupling, *refs):
        layer = own_layer(0)
        if last is None:
            (new,) = refs
        else:
            index, partials, new, sens = refs
        update_layer(layer, base, halo, diag, coupling, new)
        if last is not None:
            for k, row in enumerate(layer_sensitivity(layer, new, index, partials)):
                sens[k : k + 1, :] = row

    operands = (base, halo, diag, coupling, *(last or ()))
    shapes = [base.shape] + ([] if last is None else [(last[1].shape[0], last[0].shape[1])])
    return call(kernel, shapes, [VMEM] * len(operands), operands)


def odd_layer(odd, both, even, halo, fixed, after=(), last=None):
    def kernel(odd, both, even, halo, grad, diag, coupling, *refs):
        *refs, masked, base = refs[len(after) :]
        layer = own_layer(1)
        partner = both.at[1 - lax.axis_index("inst"), 1]
        if last is None:
            (new,) = refs
        else:
            index, partials, before, new, sens = refs
        local_terms(layer, odd, partner, even, grad, coupling, base, masked)
        update_layer(layer, base, halo, diag, coupling, new)
        if last is not None:
            for k, row in enumerate(layer_sensitivity(layer, new, index, partials)):
                sens[k : k + 1, :] = before[k : k + 1, :] + row

    operands = (odd, both, even, halo, *fixed, *after, *(last or ()))
    inst, _, radial, axial = odd.shape
    shapes = [odd.shape] + ([] if last is None else [last[2].shape])
    scratch = [pltpu.VMEM((inst, 4, radial, axial), jnp.float32), pltpu.VMEM(odd.shape, jnp.float32)]
    return call(kernel, shapes, [VMEM] * len(operands), operands, scratch)


def body(
    adjoint_start, objective_grad, diag_inverse, face_coupling, surface_index, wall_point_partials
):
    count = lax.axis_size("blocks")
    assert count % 2 == 0 and lax.axis_size("inst") == 2 and adjoint_start.shape[2] == 2
    inst, variables, _, radial, axial = adjoint_start.shape
    shape = (inst, variables, radial, axial)
    even_pairs = [(i, i ^ 1) for i in range(count)]
    odd_pairs = [(i, (((i + 1) ^ 1) - 1) % count) for i in range(count)]
    index = surface_index.reshape(1, -1)
    partials = jnp.transpose(wall_point_partials, (1, 2, 0, 3))

    def even_swap(layer):
        return lax.ppermute(layer, "blocks", even_pairs)

    def odd_swap(layer):
        return lax.ppermute(layer, "blocks", odd_pairs)

    def cores(values):
        return lax.all_gather(values, "inst", axis=0)

    def in_hbm(values):
        return pltpu.with_memory_space_constraint(values, pltpu.HBM)

    def exchange(even, odd):
        return cores(*call(pack_kernel, [(2,) + shape], [VMEM] * 2, [even, odd]))

    def local(even, odd, both):
        operands = (even, odd, both, fixed[0], fixed[2])
        masked = pltpu.VMEM((inst, 4, radial, axial), jnp.float32)
        return call(local_kernel, [shape], [VMEM] * 5, operands, [masked])[0]

    copies = [pltpu.SemaphoreType.DMA((inst + 3,))]
    start = in_hbm(adjoint_start)
    (even,) = call(first_kernel, [shape], [HBM], [start], copies)
    even_halo = even_swap(even)
    sources = (objective_grad, diag_inverse, face_coupling)
    *fixed, odd = call(
        load_kernel,
        [s.shape for s in sources] + [shape],
        [HBM] * 4 + [VMEM],
        [*map(in_hbm, sources), start, even],
        copies,
    )
    odd_halo = odd_swap(odd)
    both = exchange(even, odd)
    for sweep in range(SWEEPS - 1):
        base = local(even, odd, both)
        (new_even,) = even_layer(base, even_halo, fixed)
        even_halo = even_swap(new_even)
        (odd,) = odd_layer(odd, both, even, odd_halo, fixed, [new_even])
        odd_halo = odd_swap(odd)
        even = new_even
        both = exchange(even, odd)
    last = index, partials
    new_even, sens = even_layer(local(even, odd, both), even_halo, fixed, last)
    odd, sens = odd_layer(odd, both, even, odd_halo, fixed, (), last + (sens,))
    even = new_even
    (adjoint,) = call(join_kernel, [adjoint_start.shape], [VMEM] * 2, [even, odd], copies, HBM)
    return adjoint, sens + lax.ppermute(sens, "inst", [(0, 1), (1, 0)])


def solution(mesh):
    return jax.shard_map(
        body,
        mesh=mesh,
        in_specs=(
            P(("groups", "inst"), None, "blocks", None, None),
            P(("groups", "inst"), None, "blocks", None, None),
            P(("groups", "inst"), None, None, "blocks", None, None),
            P(("groups", "inst"), None, "blocks", None, None),
            P(("groups", "blocks")),
            P(("groups", "inst"), None, None, "blocks"),
        ),
        out_specs=(
            P(("groups", "inst"), None, "blocks", None, None),
            P(None, ("groups", "blocks")),
        ),
        check_vma=False,
    )
```

```python
import functools
import math

import jax
import jax.numpy as jnp
from jax import lax
from jax.experimental import pallas as pl
from jax.experimental.pallas import tpu as pltpu
from jax.sharding import PartitionSpec as P

SWEEPS = 4
SPECTRAL_WEIGHT = 0.25


def spectral_values(number):
    values = [0.0]
    for k in range(1, number):
        angle = math.pi * k / number
        values.append(SPECTRAL_WEIGHT * 0.5 * (-1) ** k * math.cos(angle) / math.sin(angle))
    return values


def local_terms(layer, own, partner, inner, grad, coupling, base, masked):
    inst, variables, radial, axial = own.shape
    values = spectral_values(2 * inst)
    rows = lax.broadcasted_iota(jnp.int32, (radial, axial), 0)
    lanes = lax.broadcasted_iota(jnp.int32, (radial, axial), 1)
    edges = (rows > 0, rows < radial - 1, lanes > 0, lanes < axial - 1)
    for n in range(inst):
        for d, inside in enumerate(edges):
            masked[n, d] = jnp.where(inside, coupling[n, 2 + d, layer], 0.0)
    for u in range(variables):
        cycle = [own[m, u] for m in range(inst)] + [partner[m, u] for m in range(inst)]
        for n in range(inst):
            center = cycle[n]
            total = grad[n, u, layer]
            total = total + coupling[n, 1 - layer, layer] * inner[n, u]
            total = total + masked[n, 0] * pltpu.roll(center, 1, 0)
            total = total + masked[n, 1] * pltpu.roll(center, radial - 1, 0)
            total = total + masked[n, 2] * pltpu.roll(center, 1, 1)
            total = total + masked[n, 3] * pltpu.roll(center, axial - 1, 1)
            term = values[inst] * cycle[n + inst]
            for k in range(1, inst):
                term = term + values[k] * (cycle[(n + k) % (2 * inst)] - cycle[(n - k) % (2 * inst)])
            base[n, u] = total - term


def update_layer(layer, base, halo, diag, coupling, new):
    inst, variables = base.shape[:2]
    for n in range(inst):
        weight = coupling[n, layer, layer]
        terms = [base[n, u] + weight * halo[n, u] for u in range(variables)]
        for v in range(variables):
            total = diag[n, 0, v, layer] * terms[0]
            for u in range(1, variables):
                total = total + diag[n, u, v, layer] * terms[u]
            new[n, v] = total


def layer_sensitivity(layer, values, index, partials):
    inst, variables, radial, axial = values.shape
    surface = index.shape[1]
    place = index[...]
    lane = place % axial
    row = (place // axial) % radial
    select = lax.broadcasted_iota(jnp.int32, (axial, surface), 0) == jnp.broadcast_to(lane, (axial, surface))
    select = select.astype(jnp.float32).astype(jnp.bfloat16)
    here = (lax.broadcasted_iota(jnp.int32, (radial, surface), 0) == jnp.broadcast_to(row, (radial, surface))) & (
        jnp.broadcast_to(place // (axial * radial), (radial, surface)) == layer
    )
    flat = values[...].reshape(inst * variables * radial, axial)
    high = flat.astype(jnp.bfloat16)
    rest = flat - high.astype(jnp.float32)
    middle = rest.astype(jnp.bfloat16)
    low = (rest - middle.astype(jnp.float32)).astype(jnp.bfloat16)
    picked = jnp.dot(
        jnp.concatenate([high, middle, low], axis=1),
        jnp.concatenate([select, select, select], axis=0),
        preferred_element_type=jnp.float32,
    )
    sums = [jnp.zeros((radial, surface), jnp.float32) for _ in range(partials.shape[0])]
    for n in range(inst):
        for v in range(variables):
            at = (n * variables + v) * radial
            part = picked[at : at + radial]
            for k in range(len(sums)):
                sums[k] = sums[k] + part * jnp.broadcast_to(partials[k, v, n : n + 1, :], (radial, surface))
    return [jnp.sum(jnp.where(here, s, 0.0), axis=0, keepdims=True) for s in sums]


def own_layer(side):
    odd_block = lax.axis_index("blocks") % 2
    return odd_block if side else 1 - odd_block


def copy_all(pairs, sems):
    copies = [pltpu.make_async_copy(*pair, sems.at[j]) for j, pair in enumerate(pairs)]
    for copy in copies:
        copy.start()
    for copy in copies:
        copy.wait()


def layer_of(source, side, out):
    return [(source.at[n, :, own_layer(side)], out.at[n]) for n in range(out.shape[0])]


def first_kernel(source, even, sems):
    copy_all(layer_of(source, 0, even), sems)


def load_kernel(grad, diag, coupling, source, after, grad_out, diag_out, coupling_out, odd, sems):
    pairs = [(coupling, coupling_out), (grad, grad_out), (diag, diag_out)]
    copy_all(layer_of(source, 1, odd) + pairs, sems)


def pack_kernel(even, odd, both):
    both[0] = even[...]
    both[1] = odd[...]


def join_kernel(even, odd, out, sems):
    copy_all([(layer, out.at[:, :, own_layer(side)]) for side, layer in enumerate((even, odd))], sems)


VMEM = pl.BlockSpec(memory_space=pltpu.VMEM)
HBM = pl.BlockSpec(memory_space=pltpu.HBM)
COST = pl.CostEstimate(flops=10**10, transcendentals=0, bytes_accessed=10**8)
PARAMS = pltpu.CompilerParams(vmem_limit_bytes=24 * 1024 * 1024)


def call(kernel, shapes, in_specs, operands, scratch=(), out_spec=VMEM):
    return pl.pallas_call(
        kernel,
        out_shape=[jax.ShapeDtypeStruct(s, jnp.float32) for s in shapes],
        in_specs=in_specs,
        out_specs=[out_spec] * len(shapes),
        scratch_shapes=list(scratch),
        cost_estimate=COST,
        compiler_params=PARAMS,
    )(*operands)


def local_kernel(side, own, inner, both, grad, coupling, *refs):
    base, masked = refs[-2:]
    partner = both.at[1 - lax.axis_index("inst"), side]
    local_terms(own_layer(side), own, partner, inner, grad, coupling, base, masked)


def finish_layer(side, base, halo, fixed, last=None):
    _, diag, coupling = fixed

    def kernel(base, halo, diag, coupling, *refs):
        layer = own_layer(side)
        if last is None:
            (new,) = refs
        else:
            index, partials, *before, new, sens = refs
        update_layer(layer, base, halo, diag, coupling, new)
        if last is not None:
            for k, row in enumerate(layer_sensitivity(layer, new, index, partials)):
                sens[k : k + 1, :] = before[0][k : k + 1, :] + row if before else row

    operands = (base, halo, diag, coupling, *(last or ()))
    shapes = [base.shape] + ([] if last is None else [(last[1].shape[0], last[0].shape[1])])
    return call(kernel, shapes, [VMEM] * len(operands), operands)


def odd_layer(odd, both, even, halo, fixed, after):
    def kernel(odd, both, even, halo, grad, diag, coupling, *refs):
        new, masked, base = refs[len(after) :]
        layer = own_layer(1)
        partner = both.at[1 - lax.axis_index("inst"), 1]
        local_terms(layer, odd, partner, even, grad, coupling, base, masked)
        update_layer(layer, base, halo, diag, coupling, new)

    operands = (odd, both, even, halo, *fixed, *after)
    inst, _, radial, axial = odd.shape
    scratch = [pltpu.VMEM((inst, 4, radial, axial), jnp.float32), pltpu.VMEM(odd.shape, jnp.float32)]
    return call(kernel, [odd.shape], [VMEM] * len(operands), operands, scratch)


def body(
    adjoint_start, objective_grad, diag_inverse, face_coupling, surface_index, wall_point_partials
):
    count = lax.axis_size("blocks")
    assert count % 2 == 0 and lax.axis_size("inst") == 2 and adjoint_start.shape[2] == 2
    inst, variables, _, radial, axial = adjoint_start.shape
    shape = (inst, variables, radial, axial)
    even_pairs = [(i, i ^ 1) for i in range(count)]
    odd_pairs = [(i, (((i + 1) ^ 1) - 1) % count) for i in range(count)]
    index = surface_index.reshape(1, -1)
    partials = jnp.transpose(wall_point_partials, (1, 2, 0, 3))

    def even_swap(layer):
        return lax.ppermute(layer, "blocks", even_pairs)

    def odd_swap(layer):
        return lax.ppermute(layer, "blocks", odd_pairs)

    def cores(values):
        return lax.all_gather(values, "inst", axis=0)

    def in_hbm(values):
        return pltpu.with_memory_space_constraint(values, pltpu.HBM)

    def exchange(even, odd):
        return cores(*call(pack_kernel, [(2,) + shape], [VMEM] * 2, [even, odd]))

    def local(side, own, inner, both, after=()):
        operands = (own, inner, both, fixed[0], fixed[2], *after)
        masked = pltpu.VMEM((inst, 4, radial, axial), jnp.float32)
        return call(functools.partial(local_kernel, side), [shape], [VMEM] * len(operands), operands, [masked])[0]

    copies = [pltpu.SemaphoreType.DMA((inst + 3,))]
    start = in_hbm(adjoint_start)
    (even,) = call(first_kernel, [shape], [HBM], [start], copies)
    even_halo = even_swap(even)
    sources = (objective_grad, diag_inverse, face_coupling)
    *fixed, odd = call(
        load_kernel,
        [s.shape for s in sources] + [shape],
        [HBM] * 4 + [VMEM],
        [*map(in_hbm, sources), start, even],
        copies,
    )
    odd_halo = odd_swap(odd)
    both = exchange(even, odd)
    for sweep in range(SWEEPS - 1):
        base = local(0, even, odd, both)
        (new_even,) = finish_layer(0, base, even_halo, fixed)
        even_halo = even_swap(new_even)
        (odd,) = odd_layer(odd, both, even, odd_halo, fixed, [new_even])
        odd_halo = odd_swap(odd)
        even = new_even
        both = exchange(even, odd)
    last = index, partials
    new_even, sens = finish_layer(0, local(0, even, odd, both), even_halo, fixed, last)
    odd_base = local(1, odd, even, both, [new_even])
    even = new_even
    odd, sens = finish_layer(1, odd_base, odd_halo, fixed, last + (sens,))
    (adjoint,) = call(join_kernel, [adjoint_start.shape], [VMEM] * 2, [even, odd], copies, HBM)
    return adjoint, sens + lax.ppermute(sens, "inst", [(0, 1), (1, 0)])


def solution(mesh):
    return jax.shard_map(
        body,
        mesh=mesh,
        in_specs=(
            P(("groups", "inst"), None, "blocks", None, None),
            P(("groups", "inst"), None, "blocks", None, None),
            P(("groups", "inst"), None, None, "blocks", None, None),
            P(("groups", "inst"), None, "blocks", None, None),
            P(("groups", "blocks")),
            P(("groups", "inst"), None, None, "blocks"),
        ),
        out_specs=(
            P(("groups", "inst"), None, "blocks", None, None),
            P(None, ("groups", "blocks")),
        ),
        check_vma=False,
    )
```
